512 devices in a mesh: seq: 32 (over y, x), trow: 2 (over core), tcol: 8 (over z).
Axes of the slice: x: 4, y: 8, z: 8, core: 2. Of those that a mesh axis runs over, the one named last changes fastest.
Arguments:
- tokens: bfloat16 [16384, 4096], P('seq', ('trow', 'tcol')), may hold values from -24 to 24
- norm_gain: float32 [4096], replicated, may hold values from 0.1 to 1.9
- in_weight: bfloat16 [3, 4096, 8192], P(None, None, ('trow', 'tcol')), may hold values from -0.09375 to 0.09375
- filter_taps: float32 [128, 8192], P(None, ('trow', 'tcol')), may hold values from -0.5 to 0.5
- conv_skip: float32 [8192], P(('trow', 'tcol')), may hold values from -1 to 1
- out_weight: bfloat16 [8192, 4096], P(('trow', 'tcol')), may hold values from -0.09375 to 0.09375
Outputs:
- mixer_out: bfloat16 [16384, 4096], P('seq', ('trow', 'tcol'))
The draws below stay inside these ranges and needn't reach their ends.
All inputs are finite; a program needn't handle non-finite values.
Results may differ from the reference program's by a relative error of at most 0.03.
Values may be sent and summed in bfloat16 or wider, within the bound.
A program may use at most 64 MiB of HBM per device.

```python
import math
import jax
import jax.numpy as jnp
from jax import lax

D = 4096
C = 8192
TAPS = 128
TOKENS = 16384
N_TROW = 2
N_TCOL = 8


def draw_tokens(key, part):
    first, second, third = jax.random.split(key, 3)
    base = jax.random.truncated_normal(first, -4.0, 4.0, (TOKENS, D), jnp.float32)
    row_scale = jnp.exp(jax.random.uniform(second, (TOKENS, 1), jnp.float32, math.log(0.5), math.log(2.0)))
    col_scale = jnp.exp(jax.random.uniform(third, (1, D), jnp.float32, math.log(0.3), math.log(3.0)))
    return (base * row_scale * col_scale).astype(jnp.bfloat16)


def spiked(values, own_key, source, target, shards_of, factor):
    def block_of(position):
        return (jnp.arange(values.shape[position]) // (values.shape[position] // shards_of)).reshape((-1,) + (1,) * (values.ndim - 1 - position))

    first = jax.random.permutation(own_key, shards_of)[block_of(target)]
    second = (block_of(target) + shards_of // 2) % shards_of
    return jnp.where((block_of(source) == first) | (block_of(source) == second), factor * values, values)


def block_scale(key, extent, shards, smallest, largest):
    factor_of = 1.0
    for axis_at, blocks in shards:
        draws = jax.random.uniform(jax.random.fold_in(jax.random.fold_in(key, 6), axis_at), (blocks,), jnp.float32, smallest / len(shards), largest / len(shards))
        factor_of = factor_of * jnp.repeat(jnp.exp(draws), extent[axis_at] // blocks).reshape((-1,) + (1,) * (len(extent) - 1 - axis_at))
    return factor_of


def normal_values(stream_key, dims, spread, most, shards=(), kind=jnp.bfloat16):
    values = spread * jax.random.normal(stream_key, dims, jnp.float32)
    if shards:
        values = values * block_scale(stream_key, dims, shards, -0.22, 0.18)
    return jnp.clip(values, -most, most).astype(kind)


def noise_with(key, dims, spread, reach, pieces, heavy, kind=jnp.bfloat16):
    values = spread * jax.random.normal(key, dims, jnp.float32)
    if pieces:
        values = values * block_scale(key, dims, pieces, -0.22, 0.18)
    return jnp.clip(spiked(values, jax.random.fold_in(key, 3), *heavy), -reach, reach).astype(kind)


def setup_inputs(seed: int = 0) -> dict:
    splits = jax.random.split(jax.random.key(seed), 7)
    tokens = draw_tokens(jax.random.fold_in(splits[6], 71), 0)
    norm_gain = jnp.clip(1.0 + 0.18 * jax.random.normal(splits[1], (D,), jnp.float32), 0.1, 1.9)
    in_weight = normal_values(splits[2], (3, D, C), D ** -0.5, 0.09375, ((2, 16),))
    filter_taps = normal_values(splits[3], (TAPS, C), TAPS ** -0.5, 0.5, ((1, 16),), jnp.float32)
    conv_skip = jnp.clip(jax.random.uniform(splits[4], (C,), jnp.float32, -1.0, 1.0) * block_scale(splits[4], (C,), ((0, 16),), -0.4, 0.0), -1.0, 1.0)
    out_weight = noise_with(splits[5], (C, D), C ** -0.5, 0.09375, ((0, 16),), (0, 1, 16, 2.0))
    return {"tokens": tokens, "norm_gain": norm_gain, "in_weight": in_weight, "filter_taps": filter_taps, "conv_skip": conv_skip, "out_weight": out_weight}


def reference(tokens, norm_gain, in_weight, filter_taps, conv_skip, out_weight):
    x = tokens.astype(jnp.float32)
    mean_square = lax.optimization_barrier(jnp.mean(x * x, axis=1, keepdims=True))
    normed = (x * lax.rsqrt(mean_square + 1e-06) * norm_gain).astype(jnp.bfloat16)
    query = jnp.dot(normed, in_weight[0], preferred_element_type=jnp.float32).astype(jnp.bfloat16)
    keys = jnp.dot(normed, in_weight[1], preferred_element_type=jnp.float32).astype(jnp.bfloat16)
    values = jnp.dot(normed, in_weight[2], preferred_element_type=jnp.float32).astype(jnp.bfloat16)
    mixed = (keys.astype(jnp.float32) * values.astype(jnp.float32)).astype(jnp.bfloat16)
    extended = jnp.concatenate([jnp.zeros((TAPS - 1, C), jnp.bfloat16), mixed], axis=0)

    def one_tap(step, total):
        index = jnp.asarray(step).astype(jnp.int32)
        window = lax.dynamic_slice_in_dim(extended, (TAPS - 1 - index).astype(jnp.int32), TOKENS, 0)
        weight = lax.dynamic_slice_in_dim(filter_taps, index, 1, 0)
        return total + window.astype(jnp.float32) * weight
    filtered = lax.fori_loop(0, TAPS, one_tap, jnp.zeros((TOKENS, C), jnp.float32))
    filtered = filtered + conv_skip * mixed.astype(jnp.float32)
    gated = (query.astype(jnp.float32) * filtered).astype(jnp.bfloat16)
    blocks = N_TROW * N_TCOL
    width = C // blocks

    def add_block(total, block):
        start = (block * width).astype(jnp.int32)
        part_gated = lax.dynamic_slice_in_dim(gated, start, width, 1)
        part_weight = lax.dynamic_slice_in_dim(out_weight, start, width, 0)
        rounded = jnp.dot(part_gated, part_weight, preferred_element_type=jnp.float32).astype(jnp.bfloat16)
        rounded = lax.optimization_barrier(rounded)
        return (total + rounded.astype(jnp.float32), None)
    total, unused = lax.scan(add_block, jnp.zeros((TOKENS, D), jnp.float32), jnp.arange(blocks, dtype=jnp.int32))
    return total.astype(jnp.bfloat16)
```

```python
import jax
import jax.numpy as jnp
from jax import lax
from jax.experimental import pallas as pl
from jax.experimental.pallas import tpu as pltpu
from jax.sharding import PartitionSpec as P

F32 = jnp.float32
BF16 = jnp.bfloat16
MESH = pl.DeviceIdType.MESH
EPS = 1e-06

RING = 8
ROWS = 512
HALF = 256
BLK = 256
CH = 512
TAPS = 128
PIECE = 128


def mixer_kernel(
    x_ref, gain_ref, win, taps, skip_ref, wout, out_ref,
    xg, xs, wv, wo, acc, sq, mx, tapc, gp, gbuf, hsend, hrecv, pbuf, rr, rl, sr, sl,
    right_sem, left_sem, peer_sem, got, w_sem, tap_sem, wo_sem, wo_send, wo_got,
    g_send, g_got, h_send, h_got, rr_send, rl_send, rr_got, rl_got,
):
    seq = lax.axis_index("seq")
    n_seq = lax.axis_size("seq")
    core = lax.axis_index("trow")
    z = lax.axis_index("tcol")
    other = 1 - core
    right = {"tcol": lax.rem(z + 1, RING)}
    left = {"tcol": lax.rem(z + RING - 1, RING)}
    peer = {"trow": other}
    after = {"seq": lax.rem(seq + 1, n_seq)}
    before = {"seq": lax.rem(seq + n_seq - 1, n_seq)}

    def block(on, shift):
        return on * RING + lax.rem(z + shift + RING, RING)

    slots = [(block(core, 0), block(other, 0))]
    for s in (1, 2, 3):
        slots.append((block(core, -s), block(core, s)))
        slots.append((block(other, -s), block(other, s)))
    slots.append((block(core, 4), block(other, 4)))

    def start_of(index, size):
        return pl.multiple_of(index * size, size)

    def w_copy(pair, q):
        return pltpu.make_async_copy(
            win.at[:, pl.ds(start_of(slots[pair][q], BLK), BLK), :],
            wv.at[pair, :, pl.ds(q * BLK, BLK), :],
            w_sem.at[pair, q],
        )

    def tap_copy(cb):
        return pltpu.make_async_copy(taps.at[:, pl.ds(cb * 128, 128)], tapc.at[cb], tap_sem.at[cb])

    def wo_copy(d):
        return pltpu.make_async_copy(
            wout.at[:, pl.ds(start_of(block(core, d), BLK), BLK)],
            wo.at[d, pl.ds(0, CH), :],
            wo_sem.at[d],
        )

    def remote(src, dst, send, recv, to):
        return pltpu.make_async_remote_copy(
            src_ref=src, dst_ref=dst, send_sem=send, recv_sem=recv, device_id=to, device_id_type=MESH
        )

    def wo_remote(d):
        return remote(
            wout.at[:, pl.ds(start_of(block(other, d), BLK), BLK)],
            wo.at[d, pl.ds(CH, CH), :],
            wo_send.at[d], wo_got.at[d], peer,
        )

    barrier = pltpu.get_barrier_semaphore()
    for to in (right, left, peer, after, before):
        pl.semaphore_signal(barrier, inc=1, device_id=to, device_id_type=MESH)
    for q in range(2):
        w_copy(0, q).start()
    pl.semaphore_wait(barrier, 5)

    rows_of = (pl.ds(HALF, HALF), pl.ds(0, HALF))

    def slot(h, pair, q):
        return xg.at[h, pair, :, pl.ds(q * BLK, BLK)]

    def to_right(h, s):
        src = x_ref.at[rows_of[h]] if s == 0 else slot(h, 2 * s - 1, 0)
        dst_pair, dst_q = (2 * s + 1, 0) if s < 3 else (7, 0)
        return remote(src, slot(h, dst_pair, dst_q), right_sem.at[h, s], got.at[h, dst_pair, dst_q], right)

    def to_left(h, s):
        src = x_ref.at[rows_of[h]] if s == 0 else slot(h, 2 * s - 1, 1)
        dst_pair, dst_q = (2 * s + 1, 1) if s < 3 else (7, 0)
        return remote(src, slot(h, dst_pair, dst_q), left_sem.at[h, s], got.at[h, dst_pair, dst_q], left)

    def to_peer(h, s):
        if s == 0:
            return remote(x_ref.at[rows_of[h]], slot(h, 0, 1), peer_sem.at[h, 0], got.at[h, 0, 1], peer)
        if s == 4:
            return remote(slot(h, 7, 0), slot(h, 7, 1), peer_sem.at[h, 4], got.at[h, 7, 1], peer)
        return remote(xg.at[h, 2 * s - 1], xg.at[h, 2 * s], peer_sem.at[h, s], got.at[h, 2 * s, 0], peer)

    def open_half(h):
        to_right(h, 0).start()
        to_left(h, 0).start()
        to_peer(h, 0).start()

    def arrivals(h, s):
        if s < 4:
            to_right(h, s - 1).wait_recv()
            if s < 3 or h == 0:
                to_right(h, s).start()
            to_left(h, s - 1).wait_recv()
            if s < 3 or h == 1:
                to_left(h, s).start()
        elif h == 0:
            to_right(h, 3).wait_recv()
        else:
            to_left(h, 3).wait_recv()
        to_peer(h, s).start()

    def project(h, pair):
        if h == 0:
            w_copy(pair, 0).wait()
            w_copy(pair, 1).wait()
        if pair == 0:
            xg[h, 0, :, 0:BLK] = x_ref[rows_of[h]]
            to_peer(h, 0).wait_recv()
        elif pair == 7:
            to_peer(h, 4).wait_recv()
        elif pair % 2 == 0:
            to_peer(h, pair // 2).wait_recv()

        @pl.loop(0, HALF // 32)
        def _(n):
            rows = pl.ds(pl.multiple_of(n * 32, 32), 32)
            wide = xg[h, pair, rows, :].astype(F32)
            xs[rows, :] = (wide * gp[pair : pair + 1, :]).astype(BF16)
            square = wide * wide
            square = square[:, 0:128] + square[:, 128:256] + square[:, 256:384] + square[:, 384:512]
            if pair == 0:
                sq[h, rows, :] = square
            else:
                sq[h, rows, :] += square

        @pl.loop(0, 3)
        def _(e):
            product = jnp.dot(xs[...], wv[pair, e], preferred_element_type=F32)
            if pair == 0:
                acc[e, rows_of[h], :] = product
            else:
                acc[e, rows_of[h], :] += product

    def close_half(h):
        base = HALF * (1 - h)

        @pl.loop(0, HALF // 64)
        def _(n):
            first = pl.multiple_of(base + n * 64, 64)
            rows = pl.ds(first, 64)
            total = jnp.sum(sq[h, pl.ds(pl.multiple_of(n * 64, 64), 64), :], axis=1, keepdims=True)
            scale = lax.rsqrt(total * (1.0 / (16 * BLK)) + EPS)
            keys = (acc[1, rows, :] * scale).astype(BF16).astype(F32)
            values = (acc[2, rows, :] * scale).astype(BF16).astype(F32)
            mixed = (keys * values).astype(BF16)
            acc[0, rows, :] = (acc[0, rows, :] * scale).astype(BF16).astype(F32)
            wide = mixed.astype(F32)
            for cb in range(4):
                mx[cb, pl.ds(pl.multiple_of(first + 128, 64), 64), :] = wide[:, cb * 128 : cb * 128 + 128]
            if h == 0:
                hsend[pl.ds(pl.multiple_of(n * 64, 64), 64), :] = mixed

    def halo():
        return remote(hsend.at[pl.ds(128, 128)], hrecv, h_send.at[0], h_got.at[0], after)

    def take_halo():
        halo().wait_recv()
        wide = jnp.where(seq > 0, hrecv[...].astype(F32), 0.0)
        for cb in range(4):
            mx[cb, 0:128, :] = wide[:, cb * 128 : cb * 128 + 128]

    def convolve(i, first_cb, n_cb):
        base = ROWS - PIECE * (i + 1)

        @pl.loop(0, 2 * n_cb)
        def _(n):
            cb = first_cb + n // 2
            row = pl.multiple_of(lax.rem(n, 2) * 64, 64)
            start = pl.multiple_of(base + row, 64)
            sums = [None] * 8
            for r in range(8):
                weights = [
                    jnp.broadcast_to(tapc[cb, 8 * m + r : 8 * m + r + 1, :], (8, 128)) for m in range(16)
                ]
                for w in range(-15, 8):
                    window = mx[cb, pl.ds(start + (128 + 8 * w - r), 8), :]
                    for m in range(16):
                        a = w + m
                        if 0 <= a < 8:
                            term = weights[m] * window
                            sums[a] = term if sums[a] is None else sums[a] + term
            lanes = pl.ds(pl.multiple_of(cb * 128, 128), 128)
            filtered = jnp.concatenate(sums, axis=0)
            query = acc[0, pl.ds(start, 64), lanes]
            gbuf[i, pl.ds(row, 64), lanes] = (query * filtered).astype(BF16)

    def exchange(i):
        return remote(
            gbuf.at[i, :, pl.ds(0, CH)], gbuf.at[i, :, pl.ds(CH, CH)], g_send.at[i], g_got.at[i], peer
        )

    def out_project(i):
        exchange(i).wait_recv()

        @pl.loop(0, RING)
        def _(d):
            pbuf[i, d] = jnp.dot(gbuf[i], wo[d], preferred_element_type=F32)

    def sum_right(i, d):
        return remote(sr.at[i, d - 1], rr.at[i, d - 1], rr_send.at[i, d - 1], rr_got.at[i, d - 1], right)

    def sum_left(i, d):
        return remote(sl.at[i, d - 1], rl.at[i, d - 1], rl_send.at[i, d - 1], rl_got.at[i, d - 1], left)

    def reduce_round(i, j):
        top_right = 4 if i % 2 == 0 else 3
        top_left = 7 - top_right
        d = top_right - j
        if d > 0:
            value = pbuf[i, d]
            if j > 0:
                sum_right(i, d + 1).wait_recv()
                value = value + rr[i, d].astype(F32)
            sr[i, d - 1] = value.astype(BF16)
            sum_right(i, d).start()
        d = top_left - j
        if d > 0:
            value = pbuf[i, RING - d]
            if j > 0:
                sum_left(i, d + 1).wait_recv()
                value = value + rl[i, d].astype(F32)
            sl[i, d - 1] = value.astype(BF16)
            sum_left(i, d).start()
        if j == 4:
            sum_right(i, 1).wait_recv()
            sum_left(i, 1).wait_recv()
            value = pbuf[i, 0] + rr[i, 0].astype(F32) + rl[i, 0].astype(F32)
            base = ROWS - PIECE * (i + 1)
            out_ref[base : base + PIECE, :] = value.astype(BF16)

    open_half(0)
    for pair in range(1, 8):
        for q in range(2):
            w_copy(pair, q).start()
    for cb in range(4):
        tap_copy(cb).start()
    for d in range(RING):
        wo_copy(d).start()
        wo_remote(d).start()
    for pair in range(8):
        for q in range(2):
            gp[pair : pair + 1, q * BLK : (q + 1) * BLK] = gain_ref[:, pl.ds(start_of(slots[pair][q], BLK), BLK)]
    project(0, 0)
    arrivals(0, 1)
    open_half(1)
    project(0, 1)
    arrivals(0, 2)
    project(0, 2)
    project(0, 3)
    arrivals(1, 1)
    project(1, 0)
    project(1, 1)
    arrivals(0, 3)
    project(0, 4)
    project(0, 5)
    arrivals(1, 2)
    project(1, 2)
    project(1, 3)
    arrivals(0, 4)
    project(0, 6)
    for cb in range(4):
        tap_copy(cb).wait()
        tapc[cb, 0:1, :] += skip_ref[:, cb * 128 : (cb + 1) * 128]
    arrivals(1, 3)
    project(0, 7)
    close_half(0)
    halo().start()
    project(1, 4)
    project(1, 5)
    convolve(0, 0, 2)
    arrivals(1, 4)
    convolve(0, 2, 2)
    exchange(0).start()
    project(1, 6)
    project(1, 7)
    close_half(1)
    take_halo()
    for d in range(RING):
        wo_copy(d).wait()
        wo_remote(d).wait_recv()

    out_project(0)
    reduce_round(0, 0)
    for i in (1, 2, 3):
        convolve(i, 0, 2)
        reduce_round(i - 1, 1)
        if i > 1:
            reduce_round(i - 2, 3)
        convolve(i, 2, 2)
        exchange(i).start()
        reduce_round(i - 1, 2)
        if i > 1:
            reduce_round(i - 2, 4)
        out_project(i)
        reduce_round(i, 0)
    reduce_round(3, 1)
    reduce_round(2, 3)
    reduce_round(3, 2)
    reduce_round(2, 4)
    reduce_round(3, 3)
    reduce_round(3, 4)

    for h in range(2):
        for s in range(4):
            if s < 3 or h == 0:
                to_right(h, s).wait_send()
            if s < 3 or h == 1:
                to_left(h, s).wait_send()
        for s in range(5):
            to_peer(h, s).wait_send()
    for d in range(RING):
        wo_remote(d).wait_send()
    halo().wait_send()
    for i in range(4):
        exchange(i).wait_send()
        for d in range(1, 5):
            if d < 4 or i % 2 == 0:
                sum_right(i, d).wait_send()
            if d < 4 or i % 2 == 1:
                sum_left(i, d).wait_send()


def on_device(tokens, norm_gain, in_weight, filter_taps, conv_skip, out_weight):
    vmem = pl.BlockSpec(memory_space=pltpu.VMEM)
    hbm = pl.BlockSpec(memory_space=pl.ANY)
    dma = pltpu.SemaphoreType.DMA
    return pl.pallas_call(
        mixer_kernel,
        out_shape=jax.ShapeDtypeStruct((ROWS, BLK), BF16),
        in_specs=[vmem, vmem, hbm, hbm, vmem, hbm],
        out_specs=vmem,
        scratch_shapes=[
            pltpu.VMEM((2, 8, HALF, 2 * BLK), BF16),
            pltpu.VMEM((HALF, 2 * BLK), BF16),
            pltpu.VMEM((8, 3, 2 * BLK, CH), BF16),
            pltpu.VMEM((RING, 2 * CH, BLK), BF16),
            pltpu.VMEM((3, ROWS, CH), F32),
            pltpu.VMEM((2, HALF, 128), F32),
            pltpu.VMEM((4, ROWS + 128, 128), F32),
            pltpu.VMEM((4, TAPS, 128), F32),
            pltpu.VMEM((8, 2 * BLK), F32),
            pltpu.VMEM((4, PIECE, 2 * CH), BF16),
            pltpu.VMEM((HALF, CH), BF16),
            pltpu.VMEM((128, CH), BF16),
            pltpu.VMEM((4, RING, PIECE, BLK), F32),
            pltpu.VMEM((4, 4, PIECE, BLK), BF16),
            pltpu.VMEM((4, 4, PIECE, BLK), BF16),
            pltpu.VMEM((4, 4, PIECE, BLK), BF16),
            pltpu.VMEM((4, 4, PIECE, BLK), BF16),
            dma((2, 4)), dma((2, 4)), dma((2, 5)), dma((2, 8, 2)), dma((8, 2)), dma((4,)),
            dma((8,)), dma((8,)), dma((8,)), dma((4,)), dma((4,)), dma((1,)), dma((1,)),
            dma((4, 4)), dma((4, 4)), dma((4, 4)), dma((4, 4)),
        ],
        compiler_params=pltpu.CompilerParams(
            collective_id=0, has_side_effects=True, vmem_limit_bytes=56 * 1024 * 1024
        ),
    )(tokens, norm_gain.reshape(1, -1), in_weight, filter_taps, conv_skip.reshape(1, -1), out_weight)


def solution(mesh):
    placed = (
        P("seq", ("trow", "tcol")),
        P(),
        P(None, None, ("trow", "tcol")),
        P(None, ("trow", "tcol")),
        P(("trow", "tcol")),
        P(("trow", "tcol"), None),
    )
    return jax.shard_map(
        on_device, mesh=mesh, in_specs=placed, out_specs=P("seq", ("trow", "tcol")), check_vma=False
    )
```

```python
import jax
import jax.numpy as jnp
from jax import lax
from jax.experimental import pallas as pl
from jax.experimental.pallas import tpu as pltpu
from jax.sharding import PartitionSpec as P

F32 = jnp.float32
BF16 = jnp.bfloat16
MESH = pl.DeviceIdType.MESH
EPS = 1e-06

RING = 8
ROWS = 512
HALF = 256
BLK = 256
CH = 512
TAPS = 128
PIECE = 128


def mixer_kernel(
    x_ref, gain_ref, win, taps, skip_ref, wout, out_ref,
    xg, xs, wv, wo, acc, sq, mx, sx, taps_v, tapc, gp, gbuf, hsend, hrecv, rr, rl, sr, sl,
    right_sem, left_sem, peer_sem, got, w_sem, tap_sem, wo_sem, wo_send, wo_got,
    g_send, g_got, h_send, h_got, rr_send, rl_send, rr_got, rl_got,
):
    seq = lax.axis_index("seq")
    n_seq = lax.axis_size("seq")
    core = lax.axis_index("trow")
    z = lax.axis_index("tcol")
    other = 1 - core
    right = {"tcol": lax.rem(z + 1, RING)}
    left = {"tcol": lax.rem(z + RING - 1, RING)}
    peer = {"trow": other}
    after = {"seq": lax.rem(seq + 1, n_seq)}
    before = {"seq": lax.rem(seq + n_seq - 1, n_seq)}

    def block(on, shift):
        return on * RING + lax.rem(z + shift + RING, RING)

    slots = [(block(core, 0), block(other, 0))]
    for s in (1, 2, 3):
        slots.append((block(core, -s), block(core, s)))
        slots.append((block(other, -s), block(other, s)))
    slots.append((block(core, 4), block(other, 4)))

    def start_of(index, size):
        return pl.multiple_of(index * size, size)

    def w_copy(pair, q):
        return pltpu.make_async_copy(
            win.at[:, pl.ds(start_of(slots[pair][q], BLK), BLK), :],
            wv.at[pair, :, pl.ds(q * BLK, BLK), :],
            w_sem.at[pair, q],
        )

    def tap_copy(cb):
        return pltpu.make_async_copy(taps.at[:, pl.ds(cb * 128, 128)], taps_v.at[cb], tap_sem.at[cb])

    def wo_copy(d):
        return pltpu.make_async_copy(
            wout.at[:, pl.ds(start_of(block(core, d), BLK), BLK)],
            wo.at[d, pl.ds(0, CH), :],
            wo_sem.at[d],
        )

    def remote(src, dst, send, recv, to):
        return pltpu.make_async_remote_copy(
            src_ref=src, dst_ref=dst, send_sem=send, recv_sem=recv, device_id=to, device_id_type=MESH
        )

    def wo_remote(d):
        return remote(
            wout.at[:, pl.ds(start_of(block(other, d), BLK), BLK)],
            wo.at[d, pl.ds(CH, CH), :],
            wo_send.at[d], wo_got.at[d], peer,
        )

    barrier = pltpu.get_barrier_semaphore()
    for to in (right, left, peer, after, before):
        pl.semaphore_signal(barrier, inc=1, device_id=to, device_id_type=MESH)
    for q in range(2):
        w_copy(0, q).start()
    pl.semaphore_wait(barrier, 5)

    rows_of = (pl.ds(HALF, HALF), pl.ds(0, HALF))

    def quarter(u):
        return pl.ds(ROWS - PIECE * (u + 1), PIECE)

    def slots_of(u, pair, first, count):
        rows = pl.ds(PIECE * (1 - u % 2), PIECE)
        return xg.at[u // 2, pair, rows, pl.ds(first * BLK, count * BLK)]

    def last_right(u):
        return u % 2 == 0

    def to_right(u, s):
        src = x_ref.at[quarter(u)] if s == 0 else slots_of(u, 2 * s - 1, 0, 1)
        pair = 2 * s + 1
        return remote(src, slots_of(u, pair, 0, 1), right_sem.at[u, s], got.at[u, pair, 0], right)

    def to_left(u, s):
        src = x_ref.at[quarter(u)] if s == 0 else slots_of(u, 2 * s - 1, 1, 1)
        pair, q = 2 * s + 1, (1 if s < 3 else 0)
        return remote(src, slots_of(u, pair, q, 1), left_sem.at[u, s], got.at[u, pair, q], left)

    def to_peer(u, s):
        if s == 0:
            return remote(x_ref.at[quarter(u)], slots_of(u, 0, 1, 1), peer_sem.at[u, 0], got.at[u, 0, 1], peer)
        if s == 4:
            return remote(slots_of(u, 7, 0, 1), slots_of(u, 7, 1, 1), peer_sem.at[u, 4], got.at[u, 7, 1], peer)
        return remote(
            slots_of(u, 2 * s - 1, 0, 2), slots_of(u, 2 * s, 0, 2), peer_sem.at[u, s], got.at[u, 2 * s, 0], peer
        )

    def arrivals(u, s):
        if s < 4:
            to_right(u, s - 1).wait_recv()
            if s < 3 or last_right(u):
                to_right(u, s).start()
            to_left(u, s - 1).wait_recv()
            if s < 3 or not last_right(u):
                to_left(u, s).start()
        elif last_right(u):
            to_right(u, 3).wait_recv()
        else:
            to_left(u, 3).wait_recv()
        to_peer(u, s).start()

    def project(h, pair):
        if h == 0:
            w_copy(pair, 0).wait()
            w_copy(pair, 1).wait()
        if pair == 0:
            xg[h, 0, :, 0:BLK] = x_ref[rows_of[h]]
        if pair == 7 or pair % 2 == 0:
            for u in (2 * h, 2 * h + 1):
                to_peer(u, (pair + 1) // 2).wait_recv()

        @pl.loop(0, HALF // 32)
        def _(n):
            rows = pl.ds(pl.multiple_of(n * 32, 32), 32)
            wide = xg[h, pair, rows, :].astype(F32)
            xs[rows, :] = (wide * gp[pair : pair + 1, :]).astype(BF16)
            square = wide * wide
            square = square[:, 0:128] + square[:, 128:256] + square[:, 256:384] + square[:, 384:512]
            if pair == 0:
                sq[h, rows, :] = square
            else:
                sq[h, rows, :] += square

        @pl.loop(0, 3)
        def _(e):
            product = jnp.dot(xs[...], wv[pair, e], preferred_element_type=F32)
            if pair == 0:
                acc[e, rows_of[h], :] = product
            else:
                acc[e, rows_of[h], :] += product

    def close_half(h):
        base = HALF * (1 - h)

        @pl.loop(0, HALF // 64)
        def _(n):
            first = pl.multiple_of(base + n * 64, 64)
            rows = pl.ds(first, 64)
            total = jnp.sum(sq[h, pl.ds(pl.multiple_of(n * 64, 64), 64), :], axis=1, keepdims=True)
            scale = lax.rsqrt(total * (1.0 / (16 * BLK)) + EPS)
            keys = (acc[1, rows, :] * scale).astype(BF16).astype(F32)
            values = (acc[2, rows, :] * scale).astype(BF16).astype(F32)
            mixed = (keys * values).astype(BF16)
            acc[0, rows, :] = (acc[0, rows, :] * scale).astype(BF16).astype(F32)
            wide = mixed.astype(F32)
            for cb in range(4):
                mx[cb, pl.ds(pl.multiple_of(first + 128, 64), 64), :] = wide[:, cb * 128 : cb * 128 + 128]
            if h == 0:
                hsend[pl.ds(pl.multiple_of(n * 64, 64), 64), :] = mixed

    def halo():
        return remote(hsend.at[pl.ds(128, 128)], hrecv, h_send.at[0], h_got.at[0], after)

    def take_halo():
        halo().wait_recv()
        wide = jnp.where(seq > 0, hrecv[...].astype(F32), 0.0)
        for cb in range(4):
            mx[cb, 0:128, :] = wide[:, cb * 128 : cb * 128 + 128]

    def split_taps(cb):
        tile = [taps_v[cb, 8 * m : 8 * m + 8, :] for m in range(16)]
        for k in range(4):
            even = [tile[4 * k], tile[4 * k + 2]]
            odd = [tile[4 * k + 1], tile[4 * k + 3]]
            both = [even[0] + odd[0], even[1] + odd[1]]
            for p, (low, high) in enumerate((even, odd, both)):
                for f, value in enumerate((low, high, low + high)):
                    tapc[cb, 3 * p + f, 8 * k : 8 * k + 8, :] = value

    def convolve(i, first_cb, n_cb):
        base = ROWS - PIECE * (i + 1)

        @pl.loop(first_cb, first_cb + n_cb)
        def _(cb):
            for t in range(31):
                here = mx[cb, pl.ds(base + 8 * t, 8), :]
                if t < 31:
                    sx[1, 8 * t : 8 * t + 8, :] = here + mx[cb, pl.ds(base + 8 * t + 8, 8), :]
                if t < 30:
                    sx[0, 8 * t : 8 * t + 8, :] = here + mx[cb, pl.ds(base + 8 * t + 16, 8), :]
            for t in range(29):
                sx[2, 8 * t : 8 * t + 8, :] = sx[1, 8 * t : 8 * t + 8, :] + sx[1, 8 * t + 16 : 8 * t + 24, :]

            def phase(p, with_before):
                begin = -1 if with_before else 0
                low = {c: None for c in range(begin, 4)}
                high = {c: None for c in range(-1, 4)}
                both = {c: None for c in range(begin, 4)}
                for r in range(8):
                    for f, sums in enumerate((low, high, both)):
                        weights = [
                            jnp.broadcast_to(tapc[cb, 3 * p + f, 8 * k + r : 8 * k + r + 1, :], (8, 128))
                            for k in range(4)
                        ]
                        offset = (p if p < 2 else 0) + (2 if f == 1 else 0)
                        for n in range(min(sums) - 3, 4):
                            first = 128 + 8 * (4 * n + offset) - r
                            if p < 2:
                                window = mx[cb, pl.ds(base + first, 8), :] if f < 2 else sx[0, first : first + 8, :]
                            else:
                                window = sx[1, first : first + 8, :] if f < 2 else sx[2, first : first + 8, :]
                            for k in range(4):
                                if n + k in sums:
                                    term = weights[k] * window
                                    sums[n + k] = term if sums[n + k] is None else sums[n + k] + term
                tiles = {}
                for c in range(begin, 4):
                    if c >= 0:
                        tiles[2 * c] = low[c] + high[c - 1]
                    tiles[2 * c + 1] = both[c] - low[c] - high[c]
                return tiles

            even = phase(0, False)
            odd = phase(1, True)
            both = phase(2, False)
            lanes = pl.ds(pl.multiple_of(cb * 128, 128), 128)
            for b in range(0, 8):
                pair_of = (even[b] + odd[b - 1], both[b] - even[b] - odd[b])
                filtered = jnp.concatenate(pair_of, axis=0)
                query = acc[0, base + 16 * b : base + 16 * b + 16, lanes]
                gbuf[i, 16 * b : 16 * b + 16, lanes] = (query * filtered).astype(BF16)

    def exchange(i):
        return remote(
            gbuf.at[i, :, pl.ds(0, CH)], gbuf.at[i, :, pl.ds(CH, CH)], g_send.at[i], g_got.at[i], peer
        )

    def share(i, d):
        return jnp.dot(gbuf[i], wo[d], preferred_element_type=F32)

    def sum_right(i, d):
        return remote(sr.at[i, d - 1], rr.at[i, d - 1], rr_send.at[i, d - 1], rr_got.at[i, d - 1], right)

    def sum_left(i, d):
        return remote(sl.at[i, d - 1], rl.at[i, d - 1], rl_send.at[i, d - 1], rl_got.at[i, d - 1], left)

    def reduce_round(i, j):
        top_right = 4 if i % 2 == 0 else 3
        top_left = 7 - top_right
        if j == 0:
            exchange(i).wait_recv()
        d = top_right - j
        if d > 0:
            value = share(i, d)
            if j > 0:
                sum_right(i, d + 1).wait_recv()
                value = value + rr[i, d].astype(F32)
            sr[i, d - 1] = value.astype(BF16)
            sum_right(i, d).start()
        d = top_left - j
        if d > 0:
            value = share(i, RING - d)
            if j > 0:
                sum_left(i, d + 1).wait_recv()
                value = value + rl[i, d].astype(F32)
            sl[i, d - 1] = value.astype(BF16)
            sum_left(i, d).start()
        if j == 4:
            value = share(i, 0)
            sum_right(i, 1).wait_recv()
            sum_left(i, 1).wait_recv()
            value = value + rr[i, 0].astype(F32) + rl[i, 0].astype(F32)
            base = ROWS - PIECE * (i + 1)
            out_ref[base : base + PIECE, :] = value.astype(BF16)

    for u in range(4):
        to_right(u, 0).start()
        to_left(u, 0).start()
        to_peer(u, 0).start()
    for pair in range(1, 8):
        for q in range(2):
            w_copy(pair, q).start()
    for cb in range(4):
        tap_copy(cb).start()
    for d in range(RING):
        wo_copy(d).start()
        wo_remote(d).start()
    for pair in range(8):
        for q in range(2):
            gp[pair : pair + 1, q * BLK : (q + 1) * BLK] = gain_ref[:, pl.ds(start_of(slots[pair][q], BLK), BLK)]
    project(0, 0)
    for s in range(1, 5):
        arrivals(0, s)
        project(1, 2 * s - 2)
        arrivals(1, s)
        if s < 4:
            project(0, 2 * s - 1)
        arrivals(2, s)
        project(0, 2 * s if s < 4 else 7)
        if s == 4:
            close_half(0)
            halo().start()
        arrivals(3, s)
        if s < 4:
            project(1, 2 * s - 1)
        if s == 1:
            for cb in range(4):
                tap_copy(cb).wait()
                taps_v[cb, 0:1, :] += skip_ref[:, cb * 128 : (cb + 1) * 128]
                split_taps(cb)

    convolve(0, 0, 4)
    exchange(0).start()
    project(1, 7)
    close_half(1)
    take_halo()
    for d in range(RING):
        wo_copy(d).wait()
        wo_remote(d).wait_recv()
    reduce_round(0, 0)
    convolve(1, 0, 4)
    exchange(1).start()
    reduce_round(1, 0)
    convolve(2, 0, 2)
    reduce_round(0, 1)
    convolve(2, 2, 2)
    exchange(2).start()
    reduce_round(2, 0)
    convolve(3, 0, 2)
    reduce_round(1, 1)
    reduce_round(0, 2)
    convolve(3, 2, 2)
    exchange(3).start()
    reduce_round(3, 0)
    for i, j in (
        (2, 1), (1, 2), (0, 3), (3, 1), (2, 2), (1, 3), (0, 4),
        (3, 2), (2, 3), (1, 4), (3, 3), (2, 4), (3, 4),
    ):
        reduce_round(i, j)

    for u in range(4):
        for s in range(4):
            if s < 3 or last_right(u):
                to_right(u, s).wait_send()
            if s < 3 or not last_right(u):
                to_left(u, s).wait_send()
        for s in range(5):
            to_peer(u, s).wait_send()
    for d in range(RING):
        wo_remote(d).wait_send()
    halo().wait_send()
    for i in range(4):
        exchange(i).wait_send()
        for d in range(1, 5):
            if d < 4 or i % 2 == 0:
                sum_right(i, d).wait_send()
            if d < 4 or i % 2 == 1:
                sum_left(i, d).wait_send()


def on_device(tokens, norm_gain, in_weight, filter_taps, conv_skip, out_weight):
    vmem = pl.BlockSpec(memory_space=pltpu.VMEM)
    hbm = pl.BlockSpec(memory_space=pl.ANY)
    dma = pltpu.SemaphoreType.DMA
    return pl.pallas_call(
        mixer_kernel,
        out_shape=jax.ShapeDtypeStruct((ROWS, BLK), BF16),
        in_specs=[vmem, vmem, hbm, hbm, vmem, hbm],
        out_specs=vmem,
        scratch_shapes=[
            pltpu.VMEM((2, 8, HALF, 2 * BLK), BF16),
            pltpu.VMEM((HALF, 2 * BLK), BF16),
            pltpu.VMEM((8, 3, 2 * BLK, CH), BF16),
            pltpu.VMEM((RING, 2 * CH, BLK), BF16),
            pltpu.VMEM((3, ROWS, CH), F32),
            pltpu.VMEM((2, HALF, 128), F32),
            pltpu.VMEM((4, ROWS + 128, 128), F32),
            pltpu.VMEM((3, 256, 128), F32),
            pltpu.VMEM((4, TAPS, 128), F32),
            pltpu.VMEM((4, 9, 32, 128), F32),
            pltpu.VMEM((8, 2 * BLK), F32),
            pltpu.VMEM((4, PIECE, 2 * CH), BF16),
            pltpu.VMEM((HALF, CH), BF16),
            pltpu.VMEM((128, CH), BF16),
            pltpu.VMEM((4, 4, PIECE, BLK), BF16),
            pltpu.VMEM((4, 4, PIECE, BLK), BF16),
            pltpu.VMEM((4, 4, PIECE, BLK), BF16),
            pltpu.VMEM((4, 4, PIECE, BLK), BF16),
            dma((4, 4)), dma((4, 4)), dma((4, 5)), dma((4, 8, 2)), dma((8, 2)), dma((4,)),
            dma((8,)), dma((8,)), dma((8,)), dma((4,)), dma((4,)), dma((1,)), dma((1,)),
            dma((4, 4)), dma((4, 4)), dma((4, 4)), dma((4, 4)),
        ],
        compiler_params=pltpu.CompilerParams(
            collective_id=0, has_side_effects=True, vmem_limit_bytes=56 * 1024 * 1024
        ),
    )(tokens, norm_gain.reshape(1, -1), in_weight, filter_taps, conv_skip.reshape(1, -1), out_weight)


def solution(mesh):
    placed = (
        P("seq", ("trow", "tcol")),
        P(),
        P(None, None, ("trow", "tcol")),
        P(None, ("trow", "tcol")),
        P(("trow", "tcol")),
        P(("trow", "tcol"), None),
    )
    return jax.shard_map(
        on_device, mesh=mesh, in_specs=placed, out_specs=P("seq", ("trow", "tcol")), check_vma=False
    )
```

```python
import jax
import jax.numpy as jnp
from jax import lax
from jax.experimental import pallas as pl
from jax.experimental.pallas import tpu as pltpu
from jax.sharding import PartitionSpec as P

F32 = jnp.float32
BF16 = jnp.bfloat16
MESH = pl.DeviceIdType.MESH
EPS = 1e-06

RING = 8
ROWS = 512
HALF = 256
BLK = 256
CH = 512
TAPS = 128
PIECE = 128


def mixer_kernel(
    x_ref, gain_ref, win, taps, skip_ref, wout, out_ref,
    xg, xs, wv, wo, acc, sq, mx, sx, taps_v, tapc, gp, gbuf, hsend, hrecv, rr, rl, sr, sl, gain_v, skip_v, result,
    right_sem, left_sem, peer_sem, got, w_sem, tap_sem, wo_sem, wo_send, wo_got,
    g_send, g_got, h_send, h_got, rr_send, rl_send, rr_got, rl_got, own_sem, small_sem, out_sem,
):
    seq = lax.axis_index("seq")
    n_seq = lax.axis_size("seq")
    core = lax.axis_index("trow")
    z = lax.axis_index("tcol")
    other = 1 - core
    right = {"tcol": lax.rem(z + 1, RING)}
    left = {"tcol": lax.rem(z + RING - 1, RING)}
    peer = {"trow": other}
    after = {"seq": lax.rem(seq + 1, n_seq)}
    before = {"seq": lax.rem(seq + n_seq - 1, n_seq)}

    def block(on, shift):
        return on * RING + lax.rem(z + shift + RING, RING)

    slots = [(block(core, 0), block(other, 0))]
    for s in (1, 2, 3):
        slots.append((block(core, -s), block(core, s)))
        slots.append((block(other, -s), block(other, s)))
    slots.append((block(core, 4), block(other, 4)))

    def start_of(index, size):
        return pl.multiple_of(index * size, size)

    def w_copy(pair, q):
        return pltpu.make_async_copy(
            win.at[:, pl.ds(start_of(slots[pair][q], BLK), BLK), :],
            wv.at[pair, :, pl.ds(q * BLK, BLK), :],
            w_sem.at[pair, q],
        )

    def tap_copy(cb):
        return pltpu.make_async_copy(taps.at[:, pl.ds(cb * 128, 128)], taps_v.at[cb], tap_sem.at[cb])

    def wo_copy(d):
        return pltpu.make_async_copy(
            wout.at[:, pl.ds(start_of(block(core, d), BLK), BLK)],
            wo.at[d, pl.ds(0, CH), :],
            wo_sem.at[d],
        )

    def remote(src, dst, send, recv, to):
        return pltpu.make_async_remote_copy(
            src_ref=src, dst_ref=dst, send_sem=send, recv_sem=recv, device_id=to, device_id_type=MESH
        )

    def wo_remote(d):
        return remote(
            wout.at[:, pl.ds(start_of(block(other, d), BLK), BLK)],
            wo.at[d, pl.ds(CH, CH), :],
            wo_send.at[d], wo_got.at[d], peer,
        )

    def quarter(u):
        return pl.ds(ROWS - PIECE * (u + 1), PIECE)

    def own_copy(u):
        return pltpu.make_async_copy(x_ref.at[quarter(u)], xg.at[u, 0, 0], own_sem.at[u])

    barrier = pltpu.get_barrier_semaphore()
    for to in (right, left, peer, before):
        pl.semaphore_signal(barrier, inc=1, device_id=to, device_id_type=MESH)
    local_copies = [
        pltpu.make_async_copy(gain_ref, gain_v, small_sem.at[0]),
        pltpu.make_async_copy(skip_ref, skip_v, small_sem.at[1]),
    ]
    for copy in local_copies:
        copy.start()
    for u in range(4):
        own_copy(u).start()
    for q in range(2):
        w_copy(0, q).start()
    pl.semaphore_wait(barrier, 4)

    rows_of = (pl.ds(HALF, HALF), pl.ds(0, HALF))

    def slots_of(u, pair, first, count):
        return xg.at[u, pair, first] if count == 1 else xg.at[u, pair]

    def last_right(u):
        return u % 2 == 0

    def to_right(u, s):
        src = x_ref.at[quarter(u)] if s == 0 else slots_of(u, 2 * s - 1, 0, 1)
        pair = 2 * s + 1
        return remote(src, slots_of(u, pair, 0, 1), right_sem.at[u, s], got.at[u, pair, 0], right)

    def to_left(u, s):
        src = x_ref.at[quarter(u)] if s == 0 else slots_of(u, 2 * s - 1, 1, 1)
        pair, q = 2 * s + 1, (1 if s < 3 else 0)
        return remote(src, slots_of(u, pair, q, 1), left_sem.at[u, s], got.at[u, pair, q], left)

    def to_peer(u, s):
        if s == 0:
            return remote(x_ref.at[quarter(u)], slots_of(u, 0, 1, 1), peer_sem.at[u, 0], got.at[u, 0, 1], peer)
        if s == 4:
            return remote(slots_of(u, 7, 0, 1), slots_of(u, 7, 1, 1), peer_sem.at[u, 4], got.at[u, 7, 1], peer)
        return remote(
            slots_of(u, 2 * s - 1, 0, 2), slots_of(u, 2 * s, 0, 2), peer_sem.at[u, s], got.at[u, 2 * s, 0], peer
        )

    def arrivals(u, s):
        if s < 4:
            to_right(u, s - 1).wait_recv()
            if s < 3 or last_right(u):
                to_right(u, s).start()
            to_left(u, s - 1).wait_recv()
            if s < 3 or not last_right(u):
                to_left(u, s).start()
        elif last_right(u):
            to_right(u, 3).wait_recv()
        else:
            to_left(u, 3).wait_recv()
        to_peer(u, s).start()

    def project(h, pair):
        if h == 0:
            w_copy(pair, 0).wait()
            w_copy(pair, 1).wait()
        if pair == 0:
            for u in (2 * h, 2 * h + 1):
                own_copy(u).wait()
        if pair == 7 or pair % 2 == 0:
            for u in (2 * h, 2 * h + 1):
                to_peer(u, (pair + 1) // 2).wait_recv()

        @pl.loop(0, HALF // 32)
        def _(n):
            rows = pl.ds(pl.multiple_of(n * 32, 32), 32)
            u = 2 * h + 1 - n // 4
            inner = pl.ds(pl.multiple_of(lax.rem(n, 4) * 32, 32), 32)
            square = None
            for q in range(2):
                wide = xg[u, pair, q, inner, :].astype(F32)
                xs[rows, q * BLK : (q + 1) * BLK] = (wide * gp[pair : pair + 1, q * BLK : (q + 1) * BLK]).astype(BF16)
                term = wide * wide
                term = term[:, 0:128] + term[:, 128:256]
                square = term if square is None else square + term
            if pair == 0:
                sq[h, rows, :] = square
            else:
                sq[h, rows, :] += square

        @pl.loop(0, 3)
        def _(e):
            product = jnp.dot(xs[...], wv[pair, e], preferred_element_type=F32)
            if pair == 0:
                acc[e, rows_of[h], :] = product
            else:
                acc[e, rows_of[h], :] += product

    def close_half(h):
        base = HALF * (1 - h)

        @pl.loop(0, HALF // 64)
        def _(n):
            first = pl.multiple_of(base + n * 64, 64)
            rows = pl.ds(first, 64)
            total = jnp.sum(sq[h, pl.ds(pl.multiple_of(n * 64, 64), 64), :], axis=1, keepdims=True)
            scale = lax.rsqrt(total * (1.0 / (16 * BLK)) + EPS)
            keys = (acc[1, rows, :] * scale).astype(BF16).astype(F32)
            values = (acc[2, rows, :] * scale).astype(BF16).astype(F32)
            mixed = (keys * values).astype(BF16)
            acc[0, rows, :] = (acc[0, rows, :] * scale).astype(BF16).astype(F32)
            wide = mixed.astype(F32)
            for cb in range(4):
                mx[cb, pl.ds(pl.multiple_of(first + 128, 64), 64), :] = wide[:, cb * 128 : cb * 128 + 128]
            if h == 0:
                hsend[pl.ds(pl.multiple_of(n * 64, 64), 64), :] = mixed

    def halo():
        return remote(hsend.at[pl.ds(128, 128)], hrecv, h_send.at[0], h_got.at[0], after)

    def take_halo():
        halo().wait_recv()
        wide = jnp.where(seq > 0, hrecv[...].astype(F32), 0.0)
        for cb in range(4):
            mx[cb, 0:128, :] = wide[:, cb * 128 : cb * 128 + 128]

    def split_taps(cb):
        tile = [taps_v[cb, 8 * m : 8 * m + 8, :] for m in range(16)]
        for k in range(4):
            even = [tile[4 * k], tile[4 * k + 2]]
            odd = [tile[4 * k + 1], tile[4 * k + 3]]
            both = [even[0] + odd[0], even[1] + odd[1]]
            for p, (low, high) in enumerate((even, odd, both)):
                for f, value in enumerate((low, high, low + high)):
                    tapc[cb, 3 * p + f, 8 * k : 8 * k + 8, :] = value

    def convolve(i, first_cb, n_cb):
        base = ROWS - PIECE * (i + 1)

        @pl.loop(first_cb, first_cb + n_cb)
        def _(cb):
            for t in range(31):
                here = mx[cb, pl.ds(base + 8 * t, 8), :]
                if t < 31:
                    sx[1, 8 * t : 8 * t + 8, :] = here + mx[cb, pl.ds(base + 8 * t + 8, 8), :]
                if t < 30:
                    sx[0, 8 * t : 8 * t + 8, :] = here + mx[cb, pl.ds(base + 8 * t + 16, 8), :]
            for t in range(29):
                sx[2, 8 * t : 8 * t + 8, :] = sx[1, 8 * t : 8 * t + 8, :] + sx[1, 8 * t + 16 : 8 * t + 24, :]

            def phase(p, with_before):
                begin = -1 if with_before else 0
                low = {c: None for c in range(begin, 4)}
                high = {c: None for c in range(-1, 4)}
                both = {c: None for c in range(begin, 4)}
                for r in range(8):
                    for f, sums in enumerate((low, high, both)):
                        weights = [
                            jnp.broadcast_to(tapc[cb, 3 * p + f, 8 * k + r : 8 * k + r + 1, :], (8, 128))
                            for k in range(4)
                        ]
                        offset = (p if p < 2 else 0) + (2 if f == 1 else 0)
                        for n in range(min(sums) - 3, 4):
                            first = 128 + 8 * (4 * n + offset) - r
                            if p < 2:
                                window = mx[cb, pl.ds(base + first, 8), :] if f < 2 else sx[0, first : first + 8, :]
                            else:
                                window = sx[1, first : first + 8, :] if f < 2 else sx[2, first : first + 8, :]
                            for k in range(4):
                                if n + k in sums:
                                    term = weights[k] * window
                                    sums[n + k] = term if sums[n + k] is None else sums[n + k] + term
                tiles = {}
                for c in range(begin, 4):
                    if c >= 0:
                        tiles[2 * c] = low[c] + high[c - 1]
                    tiles[2 * c + 1] = both[c] - low[c] - high[c]
                return tiles

            even = phase(0, False)
            odd = phase(1, True)
            both = phase(2, False)
            lanes = pl.ds(pl.multiple_of(cb * 128, 128), 128)
            for b in range(0, 8):
                pair_of = (even[b] + odd[b - 1], both[b] - even[b] - odd[b])
                filtered = jnp.concatenate(pair_of, axis=0)
                query = acc[0, base + 16 * b : base + 16 * b + 16, lanes]
                gbuf[i, 16 * b : 16 * b + 16, lanes] = (query * filtered).astype(BF16)

    def exchange(i):
        return remote(
            gbuf.at[i, :, pl.ds(0, CH)], gbuf.at[i, :, pl.ds(CH, CH)], g_send.at[i], g_got.at[i], peer
        )

    def share(i, d):
        return jnp.dot(gbuf[i], wo[d], preferred_element_type=F32)

    def sum_right(i, d):
        return remote(sr.at[i, d - 1], rr.at[i, d - 1], rr_send.at[i, d - 1], rr_got.at[i, d - 1], right)

    def sum_left(i, d):
        return remote(sl.at[i, d - 1], rl.at[i, d - 1], rl_send.at[i, d - 1], rl_got.at[i, d - 1], left)

    def out_copy(i):
        return pltpu.make_async_copy(result.at[i], out_ref.at[quarter(i)], out_sem.at[i])

    def reduce_round(i, j):
        top_right = 4 if i % 2 == 0 else 3
        top_left = 7 - top_right
        if j == 0:
            exchange(i).wait_recv()
        d = top_right - j
        if d > 0:
            value = share(i, d)
            if j > 0:
                sum_right(i, d + 1).wait_recv()
                value = value + rr[i, d].astype(F32)
            sr[i, d - 1] = value.astype(BF16)
            sum_right(i, d).start()
        d = top_left - j
        if d > 0:
            value = share(i, RING - d)
            if j > 0:
                sum_left(i, d + 1).wait_recv()
                value = value + rl[i, d].astype(F32)
            sl[i, d - 1] = value.astype(BF16)
            sum_left(i, d).start()
        if j == 4:
            value = share(i, 0)
            sum_right(i, 1).wait_recv()
            sum_left(i, 1).wait_recv()
            value = value + rr[i, 0].astype(F32) + rl[i, 0].astype(F32)
            result[i] = value.astype(BF16)
            out_copy(i).start()

    for u in range(4):
        to_right(u, 0).start()
        to_left(u, 0).start()
        to_peer(u, 0).start()
    for pair in range(1, 8):
        for q in range(2):
            w_copy(pair, q).start()
    for cb in range(4):
        tap_copy(cb).start()
    for d in range(RING):
        wo_copy(d).start()
        wo_remote(d).start()
    for copy in local_copies:
        copy.wait()
    for pair in range(8):
        for q in range(2):
            gp[pair : pair + 1, q * BLK : (q + 1) * BLK] = gain_v[:, pl.ds(start_of(slots[pair][q], BLK), BLK)]
    project(0, 0)
    arrivals(0, 1)
    project(1, 0)
    arrivals(1, 1)
    project(0, 1)
    arrivals(2, 1)
    project(0, 2)
    arrivals(3, 1)
    project(1, 1)
    for cb in range(4):
        tap_copy(cb).wait()
        taps_v[cb, 0:1, :] += skip_v[:, cb * 128 : (cb + 1) * 128]
        split_taps(cb)
    arrivals(0, 2)
    project(1, 2)
    arrivals(1, 2)
    project(0, 3)
    arrivals(2, 2)
    project(0, 4)
    arrivals(3, 2)
    project(1, 3)
    arrivals(0, 3)
    project(1, 4)
    arrivals(1, 3)
    project(0, 5)
    arrivals(2, 3)
    project(0, 6)
    arrivals(3, 3)
    project(1, 5)
    arrivals(0, 4)
    arrivals(1, 4)
    project(1, 6)
    project(0, 7)
    arrivals(2, 4)
    arrivals(3, 4)
    close_half(0)
    halo().start()
    convolve(0, 0, 4)
    exchange(0).start()
    project(1, 7)
    close_half(1)
    for d in range(RING):
        wo_copy(d).wait()
        wo_remote(d).wait_recv()
    reduce_round(0, 0)
    convolve(1, 0, 4)
    exchange(1).start()
    convolve(2, 0, 2)
    reduce_round(1, 0)
    convolve(2, 2, 2)
    exchange(2).start()
    reduce_round(0, 1)
    take_halo()
    convolve(3, 0, 2)
    reduce_round(2, 0)
    convolve(3, 2, 2)
    exchange(3).start()
    reduce_round(1, 1)
    reduce_round(3, 0)
    reduce_round(0, 2)
    reduce_round(2, 1)
    reduce_round(1, 2)
    reduce_round(3, 1)
    reduce_round(0, 3)
    reduce_round(2, 2)
    reduce_round(1, 3)
    reduce_round(3, 2)
    reduce_round(0, 4)
    reduce_round(2, 3)
    reduce_round(1, 4)
    reduce_round(3, 3)
    reduce_round(2, 4)
    reduce_round(3, 4)

    for u in range(4):
        for s in range(4):
            if s < 3 or last_right(u):
                to_right(u, s).wait_send()
            if s < 3 or not last_right(u):
                to_left(u, s).wait_send()
        for s in range(5):
            to_peer(u, s).wait_send()
    for d in range(RING):
        wo_remote(d).wait_send()
    halo().wait_send()
    for i in range(4):
        out_copy(i).wait()
        exchange(i).wait_send()
        for d in range(1, 5):
            if d < 4 or i % 2 == 0:
                sum_right(i, d).wait_send()
            if d < 4 or i % 2 == 1:
                sum_left(i, d).wait_send()


def on_device(tokens, norm_gain, in_weight, filter_taps, conv_skip, out_weight):
    hbm = pl.BlockSpec(memory_space=pltpu.MemorySpace.HBM)
    dma = pltpu.SemaphoreType.DMA
    return pl.pallas_call(
        mixer_kernel,
        out_shape=jax.ShapeDtypeStruct((ROWS, BLK), BF16),
        in_specs=[hbm] * 6,
        out_specs=hbm,
        scratch_shapes=[
            pltpu.VMEM((4, 8, 2, PIECE, BLK), BF16),
            pltpu.VMEM((HALF, 2 * BLK), BF16),
            pltpu.VMEM((8, 3, 2 * BLK, CH), BF16),
            pltpu.VMEM((RING, 2 * CH, BLK), BF16),
            pltpu.VMEM((3, ROWS, CH), F32),
            pltpu.VMEM((2, HALF, 128), F32),
            pltpu.VMEM((4, ROWS + 128, 128), F32),
            pltpu.VMEM((3, 256, 128), F32),
            pltpu.VMEM((4, TAPS, 128), F32),
            pltpu.VMEM((4, 9, 32, 128), F32),
            pltpu.VMEM((8, 2 * BLK), F32),
            pltpu.VMEM((4, PIECE, 2 * CH), BF16),
            pltpu.VMEM((HALF, CH), BF16),
            pltpu.VMEM((128, CH), BF16),
            pltpu.VMEM((4, 4, PIECE, BLK), BF16),
            pltpu.VMEM((4, 4, PIECE, BLK), BF16),
            pltpu.VMEM((4, 4, PIECE, BLK), BF16),
            pltpu.VMEM((4, 4, PIECE, BLK), BF16),
            pltpu.VMEM((1, 16 * BLK), F32),
            pltpu.VMEM((1, CH), F32),
            pltpu.VMEM((4, PIECE, BLK), BF16),
            dma((4, 4)), dma((4, 4)), dma((4, 5)), dma((4, 8, 2)), dma((8, 2)), dma((4,)),
            dma((8,)), dma((8,)), dma((8,)), dma((4,)), dma((4,)), dma((1,)), dma((1,)),
            dma((4, 4)), dma((4, 4)), dma((4, 4)), dma((4, 4)), dma((4,)), dma((2,)), dma((4,)),
        ],
        compiler_params=pltpu.CompilerParams(
            collective_id=0, has_side_effects=True, vmem_limit_bytes=56 * 1024 * 1024
        ),
    )(tokens, norm_gain.reshape(1, -1), in_weight, filter_taps, conv_skip.reshape(1, -1), out_weight)


def solution(mesh):
    placed = (
        P("seq", ("trow", "tcol")),
        P(),
        P(None, None, ("trow", "tcol")),
        P(None, ("trow", "tcol")),
        P(("trow", "tcol")),
        P(("trow", "tcol"), None),
    )
    return jax.shard_map(
        on_device, mesh=mesh, in_specs=placed, out_specs=P("seq", ("trow", "tcol")), check_vma=False
    )
```

```python
import jax
import jax.numpy as jnp
from jax import lax
from jax.experimental import pallas as pl
from jax.experimental.pallas import tpu as pltpu
from jax.sharding import PartitionSpec as P

F32 = jnp.float32
BF16 = jnp.bfloat16
MESH = pl.DeviceIdType.MESH
EPS = 1e-06

RING = 8
ROWS = 512
HALF = 256
BLK = 256
CH = 512
TAPS = 128
PIECE = 128


def mixer_kernel(
    x_ref, gain_ref, win, taps, skip_ref, wout, out_ref,
    xg, xs, wv, wo, acc, sq, mx, sx, taps_v, tapc, gp, gbuf, hsend, hrecv, rr, rl, sr, sl, gain_v, skip_v, result,
    right_sem, left_sem, peer_sem, got, w_sem, tap_sem, wo_sem, wo_send, wo_got,
    g_send, g_got, h_send, h_got, rr_send, rl_send, rr_got, rl_got, own_sem, small_sem, out_sem,
):
    seq = lax.axis_index("seq")
    n_seq = lax.axis_size("seq")
    core = lax.axis_index("trow")
    z = lax.axis_index("tcol")
    other = 1 - core
    right = {"tcol": lax.rem(z + 1, RING)}
    left = {"tcol": lax.rem(z + RING - 1, RING)}
    peer = {"trow": other}
    after = {"seq": lax.rem(seq + 1, n_seq)}
    before = {"seq": lax.rem(seq + n_seq - 1, n_seq)}

    def block(on, shift):
        return on * RING + lax.rem(z + shift + RING, RING)

    slots = [(block(core, 0), block(other, 0))]
    for s in (1, 2, 3):
        slots.append((block(core, -s), block(core, s)))
        slots.append((block(other, -s), block(other, s)))
    slots.append((block(core, 4), block(other, 4)))

    def start_of(index, size):
        return pl.multiple_of(index * size, size)

    def w_copy(pair, q):
        return pltpu.make_async_copy(
            win.at[:, pl.ds(start_of(slots[pair][q], BLK), BLK), :],
            wv.at[pair, :, pl.ds(q * BLK, BLK), :],
            w_sem.at[pair, q],
        )

    def tap_copy(cb):
        return pltpu.make_async_copy(taps.at[:, pl.ds(cb * 128, 128)], taps_v.at[cb], tap_sem.at[cb])

    def wo_copy(d):
        return pltpu.make_async_copy(
            wout.at[:, pl.ds(start_of(block(core, d), BLK), BLK)],
            wo.at[d, pl.ds(0, CH), :],
            wo_sem.at[d],
        )

    def remote(src, dst, send, recv, to):
        return pltpu.make_async_remote_copy(
            src_ref=src, dst_ref=dst, send_sem=send, recv_sem=recv, device_id=to, device_id_type=MESH
        )

    def wo_remote(d):
        return remote(
            wout.at[:, pl.ds(start_of(block(other, d), BLK), BLK)],
            wo.at[d, pl.ds(CH, CH), :],
            wo_send.at[d], wo_got.at[d], peer,
        )

    def quarter(u):
        return pl.ds(ROWS - PIECE * (u + 1), PIECE)

    def own_copy(u):
        return pltpu.make_async_copy(x_ref.at[quarter(u)], xg.at[u, 0, 0], own_sem.at[u])

    barrier = pltpu.get_barrier_semaphore()
    for to in (right, left, peer, before):
        pl.semaphore_signal(barrier, inc=1, device_id=to, device_id_type=MESH)
    local_copies = [
        pltpu.make_async_copy(gain_ref, gain_v, small_sem.at[0]),
        pltpu.make_async_copy(skip_ref, skip_v, small_sem.at[1]),
    ]
    for copy in local_copies:
        copy.start()
    for u in range(4):
        own_copy(u).start()
    for q in range(2):
        w_copy(0, q).start()
    pl.semaphore_wait(barrier, 4)

    rows_of = (pl.ds(HALF, HALF), pl.ds(0, HALF))

    def slots_of(u, pair, first, count):
        return xg.at[u, pair, first] if count == 1 else xg.at[u, pair]

    def last_right(u):
        return u % 2 == 0

    def to_right(u, s):
        src = x_ref.at[quarter(u)] if s == 0 else slots_of(u, 2 * s - 1, 0, 1)
        pair = 2 * s + 1
        return remote(src, slots_of(u, pair, 0, 1), right_sem.at[u, s], got.at[u, pair, 0], right)

    def to_left(u, s):
        src = x_ref.at[quarter(u)] if s == 0 else slots_of(u, 2 * s - 1, 1, 1)
        pair, q = 2 * s + 1, (1 if s < 3 else 0)
        return remote(src, slots_of(u, pair, q, 1), left_sem.at[u, s], got.at[u, pair, q], left)

    def to_peer(u, s):
        if s == 0:
            return remote(x_ref.at[quarter(u)], slots_of(u, 0, 1, 1), peer_sem.at[u, 0], got.at[u, 0, 1], peer)
        if s == 4:
            return remote(slots_of(u, 7, 0, 1), slots_of(u, 7, 1, 1), peer_sem.at[u, 4], got.at[u, 7, 1], peer)
        return remote(
            slots_of(u, 2 * s - 1, 0, 2), slots_of(u, 2 * s, 0, 2), peer_sem.at[u, s], got.at[u, 2 * s, 0], peer
        )

    def arrivals(u, s):
        if s < 4:
            to_right(u, s - 1).wait_recv()
            if s < 3 or last_right(u):
                to_right(u, s).start()
            to_left(u, s - 1).wait_recv()
            if s < 3 or not last_right(u):
                to_left(u, s).start()
        elif last_right(u):
            to_right(u, 3).wait_recv()
        else:
            to_left(u, 3).wait_recv()
        to_peer(u, s).start()

    def project(h, pair):
        if h == 0:
            w_copy(pair, 0).wait()
            w_copy(pair, 1).wait()
        if pair == 0:
            for u in (2 * h, 2 * h + 1):
                own_copy(u).wait()
        if pair == 7 or pair % 2 == 0:
            for u in (2 * h, 2 * h + 1):
                to_peer(u, (pair + 1) // 2).wait_recv()

        @pl.loop(0, HALF // 32)
        def _(n):
            rows = pl.ds(pl.multiple_of(n * 32, 32), 32)
            u = 2 * h + 1 - n // 4
            inner = pl.ds(pl.multiple_of(lax.rem(n, 4) * 32, 32), 32)
            square = None
            for q in range(2):
                wide = xg[u, pair, q, inner, :].astype(F32)
                xs[rows, q * BLK : (q + 1) * BLK] = (wide * gp[pair : pair + 1, q * BLK : (q + 1) * BLK]).astype(BF16)
                term = wide * wide
                term = term[:, 0:128] + term[:, 128:256]
                square = term if square is None else square + term
            if pair == 0:
                sq[h, rows, :] = square
            else:
                sq[h, rows, :] += square

        @pl.loop(0, 3)
        def _(e):
            product = jnp.dot(xs[...], wv[pair, e], preferred_element_type=F32)
            if pair == 0:
                acc[e, rows_of[h], :] = product
            else:
                acc[e, rows_of[h], :] += product

    def close_half(h):
        base = HALF * (1 - h)

        @pl.loop(0, HALF // 64)
        def _(n):
            first = pl.multiple_of(base + n * 64, 64)
            rows = pl.ds(first, 64)
            total = jnp.sum(sq[h, pl.ds(pl.multiple_of(n * 64, 64), 64), :], axis=1, keepdims=True)
            scale = lax.rsqrt(total * (1.0 / (16 * BLK)) + EPS)
            keys = (acc[1, rows, :] * scale).astype(BF16).astype(F32)
            values = (acc[2, rows, :] * scale).astype(BF16).astype(F32)
            mixed = (keys * values).astype(BF16)
            acc[0, rows, :] = (acc[0, rows, :] * scale).astype(BF16).astype(F32)
            wide = mixed.astype(F32)
            for cb in range(4):
                mx[cb, pl.ds(pl.multiple_of(first + 128, 64), 64), :] = wide[:, cb * 128 : cb * 128 + 128]
            if h == 0:
                hsend[pl.ds(pl.multiple_of(n * 64, 64), 64), :] = mixed

    def halo():
        return remote(hsend.at[pl.ds(128, 128)], hrecv, h_send.at[0], h_got.at[0], after)

    def take_halo():
        halo().wait_recv()
        wide = jnp.where(seq > 0, hrecv[...].astype(F32), 0.0)
        for cb in range(4):
            mx[cb, 0:128, :] = wide[:, cb * 128 : cb * 128 + 128]

    def split_taps(cb):
        tile = [taps_v[cb, 8 * m : 8 * m + 8, :] for m in range(16)]
        for k in range(4):
            even = [tile[4 * k], tile[4 * k + 2]]
            odd = [tile[4 * k + 1], tile[4 * k + 3]]
            both = [even[0] + odd[0], even[1] + odd[1]]
            for p, (low, high) in enumerate((even, odd, both)):
                for f, value in enumerate((low, high, low + high)):
                    tapc[cb, 3 * p + f, 8 * k : 8 * k + 8, :] = value

    def convolve(i, first_cb, n_cb):
        base = ROWS - PIECE * (i + 1)

        @pl.loop(first_cb, first_cb + n_cb)
        def _(cb):
            for t in range(31):
                here = mx[cb, pl.ds(base + 8 * t, 8), :]
                if t < 31:
                    sx[1, 8 * t : 8 * t + 8, :] = here + mx[cb, pl.ds(base + 8 * t + 8, 8), :]
                if t < 30:
                    sx[0, 8 * t : 8 * t + 8, :] = here + mx[cb, pl.ds(base + 8 * t + 16, 8), :]
            for t in range(29):
                sx[2, 8 * t : 8 * t + 8, :] = sx[1, 8 * t : 8 * t + 8, :] + sx[1, 8 * t + 16 : 8 * t + 24, :]

            def phase(p, with_before):
                begin = -1 if with_before else 0
                low = {c: None for c in range(begin, 4)}
                high = {c: None for c in range(-1, 4)}
                both = {c: None for c in range(begin, 4)}
                for r in range(8):
                    for f, sums in enumerate((low, high, both)):
                        weights = [
                            jnp.broadcast_to(tapc[cb, 3 * p + f, 8 * k + r : 8 * k + r + 1, :], (8, 128))
                            for k in range(4)
                        ]
                        offset = (p if p < 2 else 0) + (2 if f == 1 else 0)
                        for n in range(min(sums) - 3, 4):
                            first = 128 + 8 * (4 * n + offset) - r
                            if p < 2:
                                window = mx[cb, pl.ds(base + first, 8), :] if f < 2 else sx[0, first : first + 8, :]
                            else:
                                window = sx[1, first : first + 8, :] if f < 2 else sx[2, first : first + 8, :]
                            for k in range(4):
                                if n + k in sums:
                                    term = weights[k] * window
                                    sums[n + k] = term if sums[n + k] is None else sums[n + k] + term
                tiles = {}
                for c in range(begin, 4):
                    if c >= 0:
                        tiles[2 * c] = low[c] + high[c - 1]
                    tiles[2 * c + 1] = both[c] - low[c] - high[c]
                return tiles

            even = phase(0, False)
            odd = phase(1, True)
            both = phase(2, False)
            lanes = pl.ds(pl.multiple_of(cb * 128, 128), 128)
            for b in range(0, 8):
                pair_of = (even[b] + odd[b - 1], both[b] - even[b] - odd[b])
                filtered = jnp.concatenate(pair_of, axis=0)
                query = acc[0, base + 16 * b : base + 16 * b + 16, lanes]
                gbuf[i, 16 * b : 16 * b + 16, lanes] = (query * filtered).astype(BF16)

    def exchange(i):
        return remote(
            gbuf.at[i, :, pl.ds(0, CH)], gbuf.at[i, :, pl.ds(CH, CH)], g_send.at[i], g_got.at[i], peer
        )

    def share(i, d):
        return jnp.dot(gbuf[i], wo[d], preferred_element_type=F32)

    def parts(i):
        return 2 if i > 1 else 1

    def sum_copy(i, d, part, sends, lands, send_sem, got_sem, to):
        size = PIECE // parts(i)
        rows = pl.ds(part * size, size)
        return remote(
            sends.at[i, d - 1, rows], lands.at[i, d - 1, rows], send_sem.at[i, d - 1, part], got_sem.at[i, d - 1, part], to
        )

    def sum_right(i, d, part):
        return sum_copy(i, d, part, sr, rr, rr_send, rr_got, right)

    def sum_left(i, d, part):
        return sum_copy(i, d, part, sl, rl, rl_send, rl_got, left)

    def out_copy(i):
        return pltpu.make_async_copy(result.at[i], out_ref.at[quarter(i)], out_sem.at[i])

    def reduce_round(i, j):
        top_right = 4 if i % 2 == 0 else 3
        if j == 0:
            exchange(i).wait_recv()
        moves = []
        for top, side, sends, lands, copy in (
            (top_right, 1, sr, rr, sum_right), (7 - top_right, -1, sl, rl, sum_left)
        ):
            if top - j > 0:
                moves.append((top - j, share(i, side * (top - j) % RING), sends, lands, copy))
        if j == 4:
            value = share(i, 0)
        size = PIECE // parts(i)
        for part in range(parts(i)):
            first, last = part * size, (part + 1) * size
            for d, own, sends, lands, copy in moves:
                total = own[first:last]
                if j > 0:
                    copy(i, d + 1, part).wait_recv()
                    total = total + lands[i, d, first:last].astype(F32)
                sends[i, d - 1, first:last] = total.astype(BF16)
                copy(i, d, part).start()
            if j == 4:
                sum_right(i, 1, part).wait_recv()
                sum_left(i, 1, part).wait_recv()
                total = value[first:last] + rr[i, 0, first:last].astype(F32) + rl[i, 0, first:last].astype(F32)
                result[i, first:last] = total.astype(BF16)
        if j == 4:
            out_copy(i).start()

    for u in range(4):
        to_right(u, 0).start()
        to_left(u, 0).start()
        to_peer(u, 0).start()
    for cb in range(4):
        tap_copy(cb).start()
    for pair in range(1, 8):
        for q in range(2):
            w_copy(pair, q).start()
    for copy in local_copies:
        copy.wait()
    for pair in range(8):
        for q in range(2):
            gp[pair : pair + 1, q * BLK : (q + 1) * BLK] = gain_v[:, pl.ds(start_of(slots[pair][q], BLK), BLK)]
    project(0, 0)
    project(1, 0)
    for cb in range(4):
        tap_copy(cb).wait()
        taps_v[cb, 0:1, :] += skip_v[:, cb * 128 : (cb + 1) * 128]
        split_taps(cb)
    arrivals(0, 1)
    arrivals(1, 1)
    project(0, 1)
    arrivals(2, 1)
    project(0, 2)
    arrivals(3, 1)
    project(1, 1)
    for d in range(RING):
        wo_copy(d).start()
        wo_remote(d).start()
    arrivals(0, 2)
    project(1, 2)
    arrivals(1, 2)
    project(0, 3)
    arrivals(2, 2)
    project(0, 4)
    arrivals(3, 2)
    project(1, 3)
    arrivals(0, 3)
    project(1, 4)
    arrivals(1, 3)
    project(0, 5)
    arrivals(2, 3)
    project(0, 6)
    arrivals(3, 3)
    project(1, 5)
    arrivals(0, 4)
    arrivals(1, 4)
    project(1, 6)
    project(0, 7)
    arrivals(2, 4)
    arrivals(3, 4)
    close_half(0)
    halo().start()
    convolve(0, 0, 4)
    exchange(0).start()
    project(1, 7)
    for d in range(RING):
        wo_copy(d).wait()
        wo_remote(d).wait_recv()
    reduce_round(0, 0)
    close_half(1)
    convolve(1, 0, 4)
    exchange(1).start()
    convolve(2, 0, 2)
    reduce_round(1, 0)
    convolve(2, 2, 2)
    exchange(2).start()
    reduce_round(0, 1)
    take_halo()
    convolve(3, 0, 2)
    reduce_round(2, 0)
    convolve(3, 2, 2)
    exchange(3).start()
    reduce_round(1, 1)
    reduce_round(3, 0)
    reduce_round(0, 2)
    reduce_round(2, 1)
    reduce_round(1, 2)
    reduce_round(3, 1)
    reduce_round(0, 3)
    reduce_round(2, 2)
    reduce_round(1, 3)
    reduce_round(3, 2)
    reduce_round(0, 4)
    reduce_round(2, 3)
    reduce_round(1, 4)
    reduce_round(3, 3)
    reduce_round(2, 4)
    reduce_round(3, 4)

    for u in range(4):
        for s in range(4):
            if s < 3 or last_right(u):
                to_right(u, s).wait_send()
            if s < 3 or not last_right(u):
                to_left(u, s).wait_send()
        for s in range(5):
            to_peer(u, s).wait_send()
    for d in range(RING):
        wo_remote(d).wait_send()
    halo().wait_send()
    for i in range(4):
        out_copy(i).wait()
        exchange(i).wait_send()
        for d in range(1, 5):
            for part in range(parts(i)):
                if d < 4 or i % 2 == 0:
                    sum_right(i, d, part).wait_send()
                if d < 4 or i % 2 == 1:
                    sum_left(i, d, part).wait_send()


def on_device(tokens, norm_gain, in_weight, filter_taps, conv_skip, out_weight):
    hbm = pl.BlockSpec(memory_space=pltpu.MemorySpace.HBM)
    dma = pltpu.SemaphoreType.DMA
    return pl.pallas_call(
        mixer_kernel,
        out_shape=jax.ShapeDtypeStruct((ROWS, BLK), BF16),
        in_specs=[hbm] * 6,
        out_specs=hbm,
        scratch_shapes=[
            pltpu.VMEM((4, 8, 2, PIECE, BLK), BF16),
            pltpu.VMEM((HALF, 2 * BLK), BF16),
            pltpu.VMEM((8, 3, 2 * BLK, CH), BF16),
            pltpu.VMEM((RING, 2 * CH, BLK), BF16),
            pltpu.VMEM((3, ROWS, CH), F32),
            pltpu.VMEM((2, HALF, 128), F32),
            pltpu.VMEM((4, ROWS + 128, 128), F32),
            pltpu.VMEM((3, 256, 128), F32),
            pltpu.VMEM((4, TAPS, 128), F32),
            pltpu.VMEM((4, 9, 32, 128), F32),
            pltpu.VMEM((8, 2 * BLK), F32),
            pltpu.VMEM((4, PIECE, 2 * CH), BF16),
            pltpu.VMEM((HALF, CH), BF16),
            pltpu.VMEM((128, CH), BF16),
            pltpu.VMEM((4, 4, PIECE, BLK), BF16),
            pltpu.VMEM((4, 4, PIECE, BLK), BF16),
            pltpu.VMEM((4, 4, PIECE, BLK), BF16),
            pltpu.VMEM((4, 4, PIECE, BLK), BF16),
            pltpu.VMEM((1, 16 * BLK), F32),
            pltpu.VMEM((1, CH), F32),
            pltpu.VMEM((4, PIECE, BLK), BF16),
            dma((4, 4)), dma((4, 4)), dma((4, 5)), dma((4, 8, 2)), dma((8, 2)), dma((4,)),
            dma((8,)), dma((8,)), dma((8,)), dma((4,)), dma((4,)), dma((1,)), dma((1,)),
            dma((4, 4, 2)), dma((4, 4, 2)), dma((4, 4, 2)), dma((4, 4, 2)), dma((4,)), dma((2,)), dma((4,)),
        ],
        compiler_params=pltpu.CompilerParams(
            collective_id=0, has_side_effects=True, vmem_limit_bytes=56 * 1024 * 1024
        ),
    )(tokens, norm_gain.reshape(1, -1), in_weight, filter_taps, conv_skip.reshape(1, -1), out_weight)


def solution(mesh):
    placed = (
        P("seq", ("trow", "tcol")),
        P(),
        P(None, None, ("trow", "tcol")),
        P(None, ("trow", "tcol")),
        P(("trow", "tcol")),
        P(("trow", "tcol"), None),
    )
    return jax.shard_map(
        on_device, mesh=mesh, in_specs=placed, out_specs=P("seq", ("trow", "tcol")), check_vma=False
    )
```
